32 devices in a mesh: dp: 16 (over z, x, core), seq: 2 (over y).
Axes of the slice: x: 2, y: 2, z: 4, core: 2. Of those that a mesh axis runs over, the one named last changes fastest.
Arguments:
- tokens: bfloat16 [16, 256, 1024], P('dp', 'seq'), may hold values from -60 to 60
- norm1_gain: float32 [1024], P(('dp', 'seq')), may hold values from 0.1 to 1.9
- in_weight: bfloat16 [1024, 3, 1024], P('dp', None, 'seq'), may hold values from -0.1875 to 0.1875
- conv_weight: float32 [3, 1024], P(None, ('dp', 'seq')), may hold values from -3.5 to 3.5
- out_weight: bfloat16 [1024, 1024], P('dp', 'seq'), may hold values from -0.1875 to 0.1875
- norm2_gain: float32 [1024], P(('dp', 'seq')), may hold values from 0.1 to 1.9
- gate_up_weight: bfloat16 [1024, 2, 4608], P('dp', None, 'seq'), may hold values from -0.1875 to 0.1875
- down_weight: bfloat16 [4608, 1024], P('seq', 'dp'), may hold values from -0.1875 to 0.1875
- cotangent: bfloat16 [16, 256, 1024], P('dp', 'seq'), may hold values from -6 to 6
Outputs:
- block_output: float32 [16, 256, 1024], P('dp', 'seq')
- input_grad: float32 [16, 256, 1024], P('dp', 'seq')
- norm1_gain_grad: float32 [1024], P(('dp', 'seq'))
- in_weight_grad: float32 [1024, 3, 1024], P('dp', None, 'seq')
- conv_weight_grad: float32 [3, 1024], P(None, ('dp', 'seq'))
- out_weight_grad: float32 [1024, 1024], P('dp', 'seq')
- norm2_gain_grad: float32 [1024], P(('dp', 'seq'))
- gate_up_weight_grad: float32 [1024, 2, 4608], P('dp', None, 'seq')
- down_weight_grad: float32 [4608, 1024], P('seq', 'dp')
The draws below stay inside these ranges and needn't reach their ends.
All inputs are finite; a program needn't handle non-finite values.
Results may differ from the reference program's by a relative error of at most 0.019.
Values may be sent and summed in bfloat16 or wider, within the bound.
No kernel may reach another device: no remote copies, remote signals or barrier semaphores. Data moves between devices by JAX's collectives and lax.ppermute only.
A program may use at most 128 MiB of HBM per device.

```python
import jax
import jax.numpy as jnp
from jax import lax

D = 1024
FF = 4608
KERNEL = 3
SEQS = 16
LENGTH = 256
TOKENS = 4096


def draw_tokens(key, part):
    keys = jax.random.split(key, 3)
    col_scale = jnp.exp(jax.random.uniform(keys[2], (1, 1, D), minval=-1.2, maxval=1.2))
    base_part = jnp.clip(jax.random.normal(keys[0], (SEQS, LENGTH, D)), -4.0, 4.0)
    row_scale = jnp.exp(jax.random.uniform(keys[1], (SEQS, LENGTH, 1), minval=-1.2, maxval=1.2))
    return (base_part * row_scale * col_scale).astype(jnp.bfloat16)


def level_of(stream_key, dims, shards, least, largest):
    def one(axis_at, shards_of):
        heights = jax.random.uniform(jax.random.fold_in(jax.random.fold_in(stream_key, 6), axis_at), (shards_of,), jnp.float32, least / len(shards), largest / len(shards))
        return jnp.repeat(jnp.exp(heights), dims[axis_at] // shards_of).reshape((-1,) + (1,) * (len(dims) - axis_at - 1))

    level = one(*shards[0])
    for cut in shards[1:]:
        level = level * one(*cut)
    return level


def gaussian(key, dims, deviation, reach, cuts=(), held_as=jnp.bfloat16):
    result = jax.random.normal(key, dims, jnp.float32) * deviation
    if len(cuts) > 0:
        result = level_of(key, dims, cuts, -0.22, 0.18) * result
    return jnp.clip(result, min=-reach, max=reach).astype(held_as)


def setup_inputs(seed: int = 0) -> dict:
    key_list = jax.random.split(jax.random.key(seed), 10)
    return {
        "tokens": draw_tokens(jax.random.fold_in(key_list[9], 71), 0),
        "norm1_gain": jnp.clip(1.0 + 0.18 * jax.random.normal(key_list[1], (D,), jnp.float32), 0.1, 1.9),
        "in_weight": gaussian(key_list[2], (D, 3, D), D ** -0.5, 0.1875, ((0, 16), (2, 2))),
        "conv_weight": gaussian(key_list[3], (KERNEL, D), KERNEL ** -0.5, 3.5, ((1, 32),), jnp.float32),
        "out_weight": gaussian(key_list[4], (D, D), D ** -0.5, 0.1875, ((0, 16), (1, 2))),
        "norm2_gain": jnp.clip(1.0 + 0.18 * jax.random.normal(key_list[5], (D,), jnp.float32), 0.1, 1.9),
        "gate_up_weight": gaussian(key_list[6], (D, 2, FF), D ** -0.5, 0.1875, ((0, 16), (2, 2))),
        "down_weight": gaussian(key_list[7], (FF, D), (FF // 4) ** -0.5, 0.1875, ((0, 2), (1, 16))),
        "cotangent": gaussian(key_list[8], (SEQS, LENGTH, D), 1.0, 6.0, ((0, 16), (1, 2))),
    }


epsilon = 1e-05

def block_pass(carry_sums, pair_in, norm1_gain, in_weight, conv_weight, out_weight, norm2_gain, gate_up_weight, down_weight):
    source, cot_seq = pair_in
    resid = source.astype(jnp.float32)
    inverse_one = lax.rsqrt(lax.optimization_barrier(jnp.mean(resid * resid, axis=-1, keepdims=True)) + epsilon)
    normed_one = resid * inverse_one
    hidden_one = (normed_one * norm1_gain).astype(jnp.bfloat16)
    in_flat = in_weight.reshape(D, 3 * D)
    projected = jnp.dot(hidden_one, in_flat, preferred_element_type=jnp.float32).reshape(LENGTH, 3, D)
    b_gate = projected[:, 0]
    c_gate = projected[:, 1]
    x_value = projected[:, 2]
    gated = (b_gate * x_value).astype(jnp.bfloat16)
    extended = jnp.concatenate([jnp.zeros((KERNEL - 1, D), jnp.float32), gated.astype(jnp.float32)], axis=0)
    conv_out = jnp.zeros((LENGTH, D), jnp.float32)
    for offset in range(KERNEL):
        conv_out = conv_out + conv_weight[offset] * extended[offset:offset + LENGTH]
    mixed = (c_gate * conv_out).astype(jnp.bfloat16)
    middle = resid + jnp.dot(mixed, out_weight, preferred_element_type=jnp.float32)
    inverse_two = lax.rsqrt(lax.optimization_barrier(jnp.mean(middle * middle, axis=-1, keepdims=True)) + epsilon)
    normed_two = middle * inverse_two
    hidden_two = (normed_two * norm2_gain).astype(jnp.bfloat16)
    gu_flat = gate_up_weight.reshape(D, 2 * FF)
    both = jnp.dot(hidden_two, gu_flat, preferred_element_type=jnp.float32).reshape(LENGTH, 2, FF)
    gate_value = both[:, 0]
    up_value = both[:, 1]
    sigma = jax.nn.sigmoid(gate_value)
    swish = gate_value * sigma
    activation = (swish * up_value).astype(jnp.bfloat16)
    block_out = middle + jnp.dot(activation, down_weight, preferred_element_type=jnp.float32)
    cot_float = cot_seq.astype(jnp.float32)
    act_grad = jnp.dot(cot_seq, down_weight.T, preferred_element_type=jnp.float32)
    gate_grad = act_grad * up_value * (sigma * (1.0 + gate_value * (1.0 - sigma)))
    up_grad = act_grad * swish
    pair_grad = jnp.stack([gate_grad, up_grad], axis=1).astype(jnp.bfloat16).reshape(LENGTH, 2 * FF)
    normed2_grad = jnp.dot(pair_grad, gu_flat.T, preferred_element_type=jnp.float32)
    gate_up_sum = jnp.dot(hidden_two.T, pair_grad, preferred_element_type=jnp.float32).reshape(D, 2, FF)
    down_sum = jnp.dot(activation.T, cot_seq, preferred_element_type=jnp.float32)
    norm2_sum = lax.optimization_barrier(jnp.sum(normed2_grad * normed_two, axis=0))
    scaled_two = normed2_grad * norm2_gain
    middle_grad = cot_float + inverse_two * (scaled_two - normed_two * lax.optimization_barrier(jnp.mean(scaled_two * normed_two, axis=-1, keepdims=True)))
    middle_bf = middle_grad.astype(jnp.bfloat16)
    mixed_grad = jnp.dot(middle_bf, out_weight.T, preferred_element_type=jnp.float32)
    out_sum = jnp.dot(mixed.T, middle_bf, preferred_element_type=jnp.float32)
    cgate_grad = mixed_grad * conv_out
    conv_grad = mixed_grad * c_gate
    padded_grad = jnp.concatenate([conv_grad, jnp.zeros((KERNEL - 1, D), jnp.float32)], axis=0)
    gated_grad = jnp.zeros((LENGTH, D), jnp.float32)
    for offset in range(KERNEL):
        start = KERNEL - 1 - offset
        gated_grad = gated_grad + conv_weight[offset] * padded_grad[start:start + LENGTH]
    taps_sum = jnp.stack([lax.optimization_barrier(jnp.sum(conv_grad * extended[offset:offset + LENGTH], axis=0)) for offset in range(KERNEL)], axis=0)
    proj_grad = jnp.stack([gated_grad * x_value, cgate_grad, gated_grad * b_gate], axis=1).astype(jnp.bfloat16).reshape(LENGTH, 3 * D)
    normed1_grad = jnp.dot(proj_grad, in_flat.T, preferred_element_type=jnp.float32)
    in_sum = jnp.dot(hidden_one.T, proj_grad, preferred_element_type=jnp.float32).reshape(D, 3, D)
    norm1_sum = lax.optimization_barrier(jnp.sum(normed1_grad * normed_one, axis=0))
    scaled_one = normed1_grad * norm1_gain
    input_grad = middle_grad + inverse_one * (scaled_one - normed_one * lax.optimization_barrier(jnp.mean(scaled_one * normed_one, axis=-1, keepdims=True)))
    terms = (norm1_sum, in_sum, taps_sum, out_sum, norm2_sum, gate_up_sum, down_sum)
    new_sums = tuple((total + term for total, term in zip(carry_sums, terms)))
    return (new_sums, (block_out, input_grad))

def reference(tokens, norm1_gain, in_weight, conv_weight, out_weight, norm2_gain, gate_up_weight, down_weight, cotangent):
    start_sums = (jnp.zeros((D,), jnp.float32), jnp.zeros((D, 3, D), jnp.float32), jnp.zeros((KERNEL, D), jnp.float32), jnp.zeros((D, D), jnp.float32), jnp.zeros((D,), jnp.float32), jnp.zeros((D, 2, FF), jnp.float32), jnp.zeros((FF, D), jnp.float32))

    def one_sequence(carry_sums, pair_in):
        return block_pass(carry_sums, pair_in, norm1_gain, in_weight, conv_weight, out_weight, norm2_gain, gate_up_weight, down_weight)
    final_sums, stacked = lax.scan(one_sequence, start_sums, (tokens, cotangent))
    factor = float(TOKENS) ** (-0.5)
    norm1_sum, in_sum, taps_sum, out_sum, norm2_sum, gate_up_sum, down_sum = final_sums
    return (stacked[0], stacked[1], norm1_sum * factor, in_sum * factor, taps_sum * factor, out_sum * factor, norm2_sum * factor, gate_up_sum * factor, down_sum * factor)
```

```python
import math

import jax
import jax.numpy as jnp
from jax import lax
from jax.sharding import Mesh
from jax.sharding import PartitionSpec as P

epsilon = 1e-05
BF = jnp.bfloat16
F32 = jnp.float32
PLANE = ("x", "c", "y")
CHIPS = ("x", "y")
CELL = ("x", "c")


def size_of(axes):
    axes = (axes,) if isinstance(axes, str) else axes
    return math.prod(lax.axis_size(a) for a in axes)


def swap(block, axes, k):
    if k == 0:
        return block
    return lax.ppermute(block, axes, [(i, i ^ k) for i in range(size_of(axes))])


def pick(blocks, i):
    return lax.dynamic_index_in_dim(blocks, i, 0, keepdims=False)


def dot(a, b, dims=(1, 0)):
    return lax.dot_general(a, b, (((dims[0],), (dims[1],)), ((), ())), preferred_element_type=F32)


def exchange(blocks, axes):
    me = lax.axis_index(axes)
    n = size_of(axes)
    got = jnp.stack([swap(pick(blocks, me ^ k), axes, k) for k in range(n)])
    return [pick(got, me ^ j) for j in range(n)]


def gather_rows(rows):
    near = jnp.concatenate([swap(rows, CHIPS, k) for k in range(size_of(CHIPS))], axis=0)
    return jnp.concatenate([near, swap(near, "c", 1)], axis=0)


def scatter_rows(part):
    n = size_of(CHIPS)
    half = part.shape[0] // 2
    mine = part[:half].astype(F32) + swap(part[half:], "c", 1).astype(F32)
    mine = mine.reshape((n, half // n) + part.shape[1:])
    total = mine[0]
    sent = mine.astype(BF)
    for k in range(1, n):
        total = total + swap(sent[k], CHIPS, k).astype(F32)
    return total


def plane_exchange(blocks):
    return lax.all_to_all(blocks, PLANE, 0, 0, tiled=True)


def thirds(a):
    high = lax.reduce_precision(a, 8, 7)
    rest = a - high
    mid = lax.reduce_precision(rest, 8, 7)
    return jnp.stack([high, mid, rest - mid]).astype(BF)


def whole(parts):
    parts = parts.astype(F32)
    return parts[0] + parts[1] + parts[2]


def lane_orders(zy, cells, ny, sub):
    n = zy * cells * ny * sub
    p = jnp.arange(2 * n).reshape(2, zy, cells, ny, sub).transpose(2, 3, 0, 1, 4).reshape(-1)
    m = 2 * ny * zy * sub
    q = jnp.arange(m).reshape(ny, 2, zy * sub).transpose(1, 0, 2).reshape(-1)
    send = (jnp.arange(2 * n)[:, None] == p[None, :]).astype(BF)
    take = (jnp.arange(m)[:, None] == q[None, :]).astype(BF)
    return send, take


def local(
    tokens,
    norm1_gain,
    in_weight,
    conv_weight,
    out_weight,
    norm2_gain,
    gate_up_weight,
    down_weight,
    cotangent,
):
    nz, nx, nc, ny = (size_of(a) for a in ("z", "x", "c", "y"))
    z, y = lax.axis_index("z"), lax.axis_index("y")
    cell = lax.axis_index(CELL)
    cells = nx * nc
    members = cells * ny
    rows = in_weight.shape[0]
    half = rows // 2
    sub = rows // ny
    zy = nz // ny
    width = conv_weight.shape[0]
    rim = width - 1
    seqs, piece, model = tokens.shape
    own = seqs * piece
    plane_rows = cells * rows
    hidden = gate_up_weight.shape[2] // cells
    channels = nz * sub
    cols = in_weight.shape[2]
    lanes = 2 * zy * sub
    tok = tokens.reshape(own, model)
    cot = cotangent.reshape(own, model)
    send_order, take_order = lane_orders(zy, cells, ny, sub)

    small = jnp.concatenate([norm1_gain[None], norm2_gain[None], conv_weight], axis=0)
    kinds = small.shape[0]
    small = thirds(small).reshape(-1)
    count = small.shape[0]
    small = jnp.pad(small, (0, rows * 128 - count)).reshape(rows, 128)
    first = jnp.concatenate(
        [in_weight[:, j] for j in range(3)] + [out_weight, small], axis=1
    )
    first = lax.all_gather(first, "z", axis=0, tiled=False)

    tok_all = gather_rows(tok)

    down_rows = down_weight.T
    pieces = jnp.stack(
        [
            jnp.concatenate(
                [
                    w[:, j * hidden : (j + 1) * hidden]
                    for w in (gate_up_weight[:, 0], gate_up_weight[:, 1], down_rows)
                ],
                axis=1,
            )
            for j in range(cells)
        ]
    )
    ffn_block = jnp.concatenate(exchange(pieces, CELL), axis=0)
    gu_mine = lax.all_gather(ffn_block[:, : 2 * hidden], "z", axis=0, tiled=True)
    down_t = lax.all_gather(ffn_block[:, 2 * hidden :], "z", axis=0, tiled=True)
    gate_w = gu_mine[:, :hidden]
    up_w = gu_mine[:, hidden:]

    cot_all = gather_rows(cot)

    raw = first[:, :, : 3 * cols].reshape(nz, 2, half, 3, cols)
    raw = raw.transpose(3, 0, 2, 1, 4).reshape(3 * nz * half, 2 * cols)
    sent = dot(raw, send_order).astype(BF).reshape(3 * nz * half, members, lanes)
    sent = sent.transpose(1, 0, 2)
    held = first[:, :, 3 * cols + model // ny :].reshape(nz, rows * 128)[:, :count].reshape(-1)
    extra = -(-nz * count // lanes)
    extra = -(-extra // 16) * 16
    held = jnp.pad(held, (0, extra * lanes - nz * count)).reshape(1, extra, lanes)
    sent = jnp.concatenate([sent, jnp.broadcast_to(held, (members, extra, lanes))], axis=1)
    came = plane_exchange(sent)
    held = came[:, 3 * nz * half :].reshape(members, -1)[:, : nz * count]
    held = held.reshape(members, nz, 3, kinds, sub).transpose(2, 3, 1, 0, 4)
    held = whole(held)
    gain_one = held[0].reshape(model)
    gain_two = held[1].reshape(model)
    taps = lax.dynamic_index_in_dim(held[2:], cell * ny + y, 2, keepdims=False)
    taps = taps.reshape(width, channels)
    came = came[:, : 3 * nz * half].reshape(cells, ny, 3 * nz * half, lanes)
    came = came.transpose(0, 2, 1, 3).reshape(cells * 3 * nz * half, ny * lanes)
    came = dot(came, take_order).astype(BF).reshape(cells, 3, nz, half, 2, channels)
    in_mine = came.transpose(2, 0, 4, 3, 1, 5).reshape(model, 3 * channels)
    out_raw = first[:, :, 3 * cols : 3 * cols + model // ny].reshape(nz, ny, sub, model // ny)
    out_raw = out_raw.transpose(1, 0, 2, 3).reshape(ny, channels, model // ny)
    out_mine = jnp.concatenate(exchange(out_raw, "y"), axis=1)

    resid_all = tok_all.astype(F32)
    inv_all = lax.rsqrt(jnp.mean(resid_all * resid_all, axis=-1, keepdims=True) + epsilon)
    hidden_one = (resid_all * inv_all * gain_one).astype(BF)
    proj = dot(hidden_one, in_mine)
    b_gate = proj[:, :channels]
    c_gate = proj[:, channels : 2 * channels]
    x_value = proj[:, 2 * channels :]
    gated = (b_gate * x_value).astype(BF)

    groups = (nc * nx, ny, seqs, piece, channels)

    def from_piece(a, at, by):
        rows_of = a.reshape(groups)[:, :, :, at : at + rim]
        out = []
        for r in range(ny):
            v = jnp.zeros_like(rows_of[:, 0])
            for j in range(ny):
                v = jnp.where((y ^ r) + by == (y ^ j), rows_of[:, j], v)
            out.append(v)
        return jnp.stack(out, axis=1)

    extended = jnp.concatenate(
        [from_piece(gated, piece - rim, -1), gated.reshape(groups)], axis=3
    ).astype(F32)
    conv = jnp.zeros(groups, F32)
    for offset in range(width):
        conv = conv + taps[offset] * extended[:, :, :, offset : offset + piece]
    conv = conv.reshape(-1, channels)
    mixed = (c_gate * conv).astype(BF)
    resid = tok.astype(F32)
    inv_one = lax.rsqrt(jnp.mean(resid * resid, axis=-1, keepdims=True) + epsilon)
    middle = resid + scatter_rows(dot(mixed, out_mine).astype(BF))
    inv_two = lax.rsqrt(jnp.mean(middle * middle, axis=-1, keepdims=True) + epsilon)
    normed_two = middle * inv_two
    hidden_two = (normed_two * gain_two).astype(BF)
    rows_all = gather_rows(hidden_two)

    gate = dot(rows_all, gate_w)
    up = dot(rows_all, up_w)
    sigma = jax.nn.sigmoid(gate)
    swish = gate * sigma
    activation = (swish * up).astype(BF)
    down_term = dot(cot_all, activation, (0, 0)).astype(BF)
    down_sum = lax.psum_scatter(down_term, "z", scatter_dimension=0, tiled=True)
    act_grad = dot(cot_all, down_t)
    gate_grad = (act_grad * up * (sigma * (1.0 + gate * (1.0 - sigma)))).astype(BF)
    up_grad = (act_grad * swish).astype(BF)
    rows_grad = dot(gate_grad, gate_w, (1, 1)) + dot(up_grad, up_w, (1, 1))
    normed2_grad = scatter_rows(rows_grad.astype(BF))
    gu_term = jnp.concatenate(
        [dot(rows_all, gate_grad, (0, 0)).astype(BF), dot(rows_all, up_grad, (0, 0)).astype(BF)],
        axis=1,
    )
    gu_sum = lax.psum_scatter(gu_term, "z", scatter_dimension=0, tiled=True)
    block_out = middle + scatter_rows(dot(activation, down_t, (1, 1)).astype(BF))

    scaled_two = normed2_grad * gain_two
    middle_grad = cot.astype(F32) + inv_two * (
        scaled_two - normed_two * jnp.mean(scaled_two * normed_two, axis=-1, keepdims=True)
    )
    middle_all = gather_rows(middle_grad.astype(BF))

    mixed_grad = dot(middle_all, out_mine, (1, 1))
    out_term = dot(mixed, middle_all, (0, 0)).astype(BF)
    cgate_grad = mixed_grad * conv
    conv_grad = mixed_grad * c_gate
    padded = jnp.concatenate([conv_grad.reshape(groups), from_piece(conv_grad, 0, 1)], axis=3)
    gated_grad = jnp.zeros(groups, F32)
    for offset in range(width):
        begin = rim - offset
        gated_grad = gated_grad + taps[offset] * padded[:, :, :, begin : begin + piece]
    gated_grad = gated_grad.reshape(-1, channels)
    taps_term = jnp.stack(
        [
            jnp.sum(
                conv_grad.reshape(groups) * extended[:, :, :, offset : offset + piece],
                axis=(0, 1, 2, 3),
            )
            for offset in range(width)
        ]
    )
    proj_grad = jnp.concatenate(
        [
            (gated_grad * x_value).astype(BF),
            cgate_grad.astype(BF),
            (gated_grad * b_gate).astype(BF),
        ],
        axis=1,
    )
    in_term = dot(hidden_one, proj_grad, (0, 0)).astype(BF)
    out_term = out_term.reshape(nz, sub, members, model // members)
    out_term = out_term.transpose(0, 2, 1, 3).reshape(nz, plane_rows, model // members)
    out_width = model // members
    taps_term = taps_term.reshape(width, nz, sub).transpose(1, 0, 2)
    taps_term = jnp.pad(
        taps_term.astype(BF), ((0, 0), (0, 16 - width), (0, 3 * channels + out_width - sub))
    )
    last = jnp.concatenate([in_term.reshape(nz, plane_rows, 3 * channels), out_term], axis=2)
    last = jnp.concatenate([last, taps_term], axis=1)
    last = lax.psum_scatter(last, "z", scatter_dimension=0, tiled=True)[0]
    normed1_grad = scatter_rows(dot(proj_grad, in_mine, (1, 1)).astype(BF))
    normed_one = resid * inv_one
    scaled_one = normed1_grad * gain_one
    input_grad = middle_grad + inv_one * (
        scaled_one - normed_one * jnp.mean(scaled_one * normed_one, axis=-1, keepdims=True)
    )

    factor = 1.0 / math.sqrt(own * nz * members)
    came = exchange(down_sum.reshape(cells, rows, hidden), CELL)
    down_out = jnp.concatenate(came, axis=1).T.astype(F32) * factor
    came = exchange(gu_sum.reshape(cells, rows, 2 * hidden), CELL)
    gu_out = jnp.stack(
        [
            jnp.concatenate([b[:, :hidden] for b in came], axis=1),
            jnp.concatenate([b[:, hidden:] for b in came], axis=1),
        ],
        axis=1,
    )
    gu_out = gu_out.astype(F32) * factor
    in_sum = last[:plane_rows, : 3 * channels]
    out_sum = last[:plane_rows, 3 * channels :].reshape(ny, cells, sub, out_width)
    out_sum = out_sum.transpose(0, 2, 1, 3).reshape(ny, sub, model // ny)
    out_out = jnp.concatenate(exchange(out_sum, "y"), axis=0).astype(F32) * factor
    taps_out = last[plane_rows : plane_rows + width, :sub].astype(F32) * factor

    start = z * plane_rows
    norm1_rows = jnp.sum(
        in_sum.astype(F32)
        * lax.dynamic_slice_in_dim(in_mine, start, plane_rows, 0).astype(F32),
        axis=1,
    ) / lax.dynamic_slice_in_dim(gain_one, start, plane_rows, 0)
    norm2_rows = jnp.sum(
        gu_sum.astype(F32) * ffn_block[:, : 2 * hidden].astype(F32), axis=1
    ) / lax.dynamic_slice_in_dim(gain_two, start, plane_rows, 0)
    norm_rows = jnp.stack([norm1_rows, norm2_rows]).reshape(2, cells, rows).transpose(1, 0, 2)
    norm_rows = thirds(norm_rows).transpose(1, 0, 2, 3).reshape(cells, 1, 6 * rows)
    extra = -(-6 * rows // lanes)
    extra = -(-extra // 16) * 16
    norm_rows = jnp.pad(norm_rows, ((0, 0), (0, 0), (0, extra * lanes - 6 * rows)))
    norm_rows = jnp.broadcast_to(norm_rows, (cells, ny, extra * lanes))
    norm_rows = norm_rows.reshape(members, extra, lanes)
    sent = in_sum.reshape(cells, 2, half, 3, channels).transpose(0, 3, 2, 1, 4)
    sent = dot(sent.reshape(cells * 3 * half, 2 * channels), take_order, (1, 1)).astype(BF)
    sent = sent.reshape(cells, 3 * half, ny, lanes).transpose(0, 2, 1, 3)
    sent = sent.reshape(members, 3 * half, lanes)
    came = plane_exchange(jnp.concatenate([sent, norm_rows], axis=1))
    norm_out = came[:, 3 * half :].reshape(members, extra * lanes)[:, : 6 * rows]
    norm_out = jnp.sum(norm_out.astype(F32).reshape(members * 3, 2, rows), axis=0)
    norm_out = lax.dynamic_slice_in_dim(norm_out, y * sub, sub, 1) * factor
    came = came[:, : 3 * half].transpose(1, 0, 2).reshape(3 * half, members * lanes)
    in_out = dot(came, send_order, (1, 1)).reshape(3, half, 2, cols)
    in_out = in_out.transpose(2, 1, 0, 3).reshape(rows, 3, cols) * factor

    return (
        block_out.reshape(tokens.shape),
        input_grad.reshape(tokens.shape),
        norm_out[0],
        in_out,
        taps_out,
        out_out,
        norm_out[1],
        gu_out,
        down_out,
    )


def solution(mesh):
    dp, seq = mesh.shape["dp"], mesh.shape["seq"]
    fine = Mesh(mesh.devices.reshape(dp // 4, 2, 2, seq), ("z", "x", "c", "y"))
    dp = ("z", "x", "c")
    every = ("z", "x", "c", "y")
    return jax.shard_map(
        local,
        mesh=fine,
        in_specs=(
            P(dp, "y", None),
            P(every),
            P(dp, None, "y"),
            P(None, every),
            P(dp, "y"),
            P(every),
            P(dp, None, "y"),
            P("y", dp),
            P(dp, "y", None),
        ),
        out_specs=(
            P(dp, "y", None),
            P(dp, "y", None),
            P(every),
            P(dp, None, "y"),
            P(None, every),
            P(dp, "y"),
            P(every),
            P(dp, None, "y"),
            P("y", dp),
        ),
        check_vma=False,
    )
```

```python
import math

import jax
import jax.numpy as jnp
from jax import lax
from jax.experimental.layout import Layout, with_layout_constraint
from jax.sharding import Mesh
from jax.sharding import PartitionSpec as P

epsilon = 1e-05
BF = jnp.bfloat16
F32 = jnp.float32
PLANE = ("x", "c", "y")
CHIPS = ("x", "y")
CELL = ("x", "c")


def size_of(axes):
    axes = (axes,) if isinstance(axes, str) else axes
    return math.prod(lax.axis_size(a) for a in axes)


def swap(block, axes, k):
    if k == 0:
        return block
    return lax.ppermute(block, axes, [(i, i ^ k) for i in range(size_of(axes))])


def pick(blocks, i):
    return lax.dynamic_index_in_dim(blocks, i, 0, keepdims=False)


def dot(a, b, dims=(1, 0)):
    return lax.dot_general(a, b, (((dims[0],), (dims[1],)), ((), ())), preferred_element_type=F32)


def exchange(blocks, axes):
    me = lax.axis_index(axes)
    n = size_of(axes)
    got = jnp.stack([swap(pick(blocks, me ^ k), axes, k) for k in range(n)])
    return [pick(got, me ^ j) for j in range(n)]


def rowwise(a):
    return with_layout_constraint(a, Layout(major_to_minor=(0, 1)))


def gather_rows(rows, beside=None):
    blocks = [swap(rows, CHIPS, k) for k in range(size_of(CHIPS))]
    if beside is not None:
        blocks, beside = lax.optimization_barrier((blocks, beside))
    near = lax.optimization_barrier(rowwise(jnp.concatenate(blocks, axis=0)))
    rows = jnp.concatenate([near, swap(near, "c", 1)], axis=0)
    return rows if beside is None else (rows, beside)


def cross(part):
    return swap(rowwise(part)[part.shape[0] // 2 :], "c", 1)


def near_sums(part, far):
    n = size_of(CHIPS)
    half = part.shape[0] // 2
    mine = part[:half].astype(F32) + far.astype(F32)
    mine = mine.reshape((n, half // n) + part.shape[1:])
    return [mine[0]] + [mine[k].astype(BF) for k in range(1, n)]


def send_rows(part, far):
    mine = near_sums(part, far)
    return mine[0], [swap(mine[k], CHIPS, k) for k in range(1, len(mine))]


def add_rows(mine, came):
    for block in came:
        mine = mine + block.astype(F32)
    return mine


def scatter_rows(part):
    return add_rows(*send_rows(part, cross(part)))


def plane_exchange(blocks):
    return lax.all_to_all(blocks, PLANE, 0, 0, tiled=True)


def thirds(a):
    high = lax.reduce_precision(a, 8, 7)
    rest = a - high
    mid = lax.reduce_precision(rest, 8, 7)
    return jnp.stack([high, mid, rest - mid]).astype(BF)


def whole(parts):
    parts = parts.astype(F32)
    return parts[0] + parts[1] + parts[2]


def lane_orders(zy, cells, ny, sub):
    n = zy * cells * ny * sub
    p = jnp.arange(2 * n).reshape(2, zy, cells, ny, sub).transpose(2, 3, 0, 1, 4).reshape(-1)
    m = 2 * ny * zy * sub
    q = jnp.arange(m).reshape(ny, 2, zy * sub).transpose(1, 0, 2).reshape(-1)
    send = (jnp.arange(2 * n)[:, None] == p[None, :]).astype(BF)
    take = (jnp.arange(m)[:, None] == q[None, :]).astype(BF)
    return send, take


def local(
    tokens,
    norm1_gain,
    in_weight,
    conv_weight,
    out_weight,
    norm2_gain,
    gate_up_weight,
    down_weight,
    cotangent,
):
    nz, nx, nc, ny = (size_of(a) for a in ("z", "x", "c", "y"))
    z, y = lax.axis_index("z"), lax.axis_index("y")
    cell = lax.axis_index(CELL)
    cells = nx * nc
    members = cells * ny
    rows = in_weight.shape[0]
    half = rows // 2
    sub = rows // ny
    zy = nz // ny
    width = conv_weight.shape[0]
    rim = width - 1
    seqs, piece, model = tokens.shape
    own = seqs * piece
    plane_rows = cells * rows
    hidden = gate_up_weight.shape[2] // cells
    channels = nz * sub
    cols = in_weight.shape[2]
    lanes = 2 * zy * sub
    tok = tokens.reshape(own, model)
    cot = cotangent.reshape(own, model)
    send_order, take_order = lane_orders(zy, cells, ny, sub)

    small = jnp.concatenate([norm1_gain[None], norm2_gain[None], conv_weight], axis=0)
    kinds = small.shape[0]
    small = thirds(small).reshape(-1)
    count = small.shape[0]
    extra = -(-count // (16 * lanes)) * 16
    small = jnp.pad(small, (0, extra * lanes - count)).reshape(1, extra, lanes)
    raw = in_weight.reshape(2, half, 3, cols).transpose(2, 1, 0, 3).reshape(3 * half, 2 * cols)
    sent = dot(raw, send_order).astype(BF).reshape(3 * half, members, lanes)
    sent = sent.transpose(1, 0, 2)
    sent = jnp.concatenate([sent, jnp.broadcast_to(small, (members, extra, lanes))], axis=1)
    with jax.named_scope("inmove"):
        came = plane_exchange(sent)
    held = came[:, 3 * half :].reshape(members, extra * lanes)[:, :count].reshape(-1)
    came = came[:, : 3 * half].reshape(cells, ny, 3 * half, lanes)
    came = came.transpose(0, 2, 1, 3).reshape(cells * 3 * half, ny * lanes)
    came = dot(came, take_order).astype(BF).reshape(cells, 3, half, 2, channels)
    in_block = came.transpose(0, 3, 2, 1, 4).reshape(plane_rows, 3 * channels)
    out_width = model // members
    out_block = exchange(out_weight.reshape(ny, sub, model // ny), "y")
    out_block = jnp.concatenate(
        [b[:, j * out_width : (j + 1) * out_width] for b in out_block for j in range(cells)], axis=0
    )
    first = jnp.concatenate([in_block, out_block], axis=1)
    wide = first.shape[1]
    rest = -(-members * count // (16 * wide)) * 16
    held = jnp.pad(held, (0, rest * wide - members * count)).reshape(rest, wide)
    first = jnp.concatenate([first, held], axis=0)
    with jax.named_scope("firstmove"):
        first = lax.all_gather(first, "z", axis=0, tiled=False)

    with jax.named_scope("tokmove"):
        tok_all = gather_rows(tok)

    down_rows = down_weight.T
    pieces = jnp.stack(
        [
            jnp.concatenate(
                [
                    w[:, j * hidden : (j + 1) * hidden]
                    for w in (gate_up_weight[:, 0], gate_up_weight[:, 1], down_rows)
                ],
                axis=1,
            )
            for j in range(cells)
        ]
    )
    ffn_block = jnp.concatenate(exchange(pieces, CELL), axis=0)
    gu_block, down_block, tok_all = lax.optimization_barrier(
        (ffn_block[:, : 2 * hidden], ffn_block[:, 2 * hidden :], tok_all)
    )
    gu_mine = lax.all_gather(gu_block, "z", axis=0, tiled=True)
    down_t = lax.all_gather(down_block, "z", axis=0, tiled=True)

    with jax.named_scope("cotmove"):
        cot_all = gather_rows(cot)
    held = first[:, plane_rows:].reshape(nz, rest * wide)[:, : members * count]
    held = held.reshape(nz, members, 3, kinds, sub).transpose(2, 3, 0, 1, 4)
    held = whole(held)
    gain_one = held[0].reshape(model)
    gain_two = held[1].reshape(model)
    taps = lax.dynamic_index_in_dim(held[2:], cell * ny + y, 2, keepdims=False)
    taps = taps.reshape(width, channels)
    in_mine = first[:, :plane_rows, : 3 * channels].reshape(model, 3 * channels)
    out_mine = first[:, :plane_rows, 3 * channels :].reshape(nz, members, sub, out_width)
    out_mine = out_mine.transpose(0, 2, 1, 3).reshape(channels, model)

    resid_all = tok_all.astype(F32)
    inv_all = lax.rsqrt(jnp.mean(resid_all * resid_all, axis=-1, keepdims=True) + epsilon)
    hidden_one = (resid_all * inv_all * gain_one).astype(BF)
    proj = dot(hidden_one, in_mine)
    b_gate = proj[:, :channels]
    c_gate = proj[:, channels : 2 * channels]
    x_value = proj[:, 2 * channels :]
    gated = (b_gate * x_value).astype(BF)

    groups = (nc * nx, ny, seqs, piece, channels)

    def from_piece(a, at, by):
        rows_of = a.reshape(groups)[:, :, :, at : at + rim]
        out = []
        for r in range(ny):
            v = jnp.zeros_like(rows_of[:, 0])
            for j in range(ny):
                v = jnp.where((y ^ r) + by == (y ^ j), rows_of[:, j], v)
            out.append(v)
        return jnp.stack(out, axis=1)

    extended = jnp.concatenate(
        [from_piece(gated, piece - rim, -1), gated.reshape(groups)], axis=3
    ).astype(F32)
    conv = jnp.zeros(groups, F32)
    for offset in range(width):
        conv = conv + taps[offset] * extended[:, :, :, offset : offset + piece]
    conv = conv.reshape(-1, channels)
    mixed = (c_gate * conv).astype(BF)
    resid = tok.astype(F32)
    inv_one = lax.rsqrt(jnp.mean(resid * resid, axis=-1, keepdims=True) + epsilon)
    middle = resid + scatter_rows(dot(mixed, out_mine).astype(BF))
    inv_two = lax.rsqrt(jnp.mean(middle * middle, axis=-1, keepdims=True) + epsilon)
    normed_two = middle * inv_two
    hidden_two = (normed_two * gain_two).astype(BF)
    rows_all = gather_rows(hidden_two)

    both = dot(rows_all, gu_mine)
    gate = both[:, :hidden]
    up = both[:, hidden:]
    sigma = jax.nn.sigmoid(gate)
    swish = gate * sigma
    activation = lax.optimization_barrier((swish * up).astype(BF))
    down_term = dot(cot_all, activation, (0, 0)).astype(BF)
    down_t, down_term = lax.optimization_barrier((down_t, down_term))
    down_sum = lax.psum_scatter(down_term, "z", scatter_dimension=0, tiled=True)
    act_grad = dot(cot_all, down_t)
    gate_grad = (act_grad * up * (sigma * (1.0 + gate * (1.0 - sigma)))).astype(BF)
    up_grad = (act_grad * swish).astype(BF)
    pair_grad = jnp.concatenate([gate_grad, up_grad], axis=1)
    rows_grad = dot(pair_grad, gu_mine, (1, 1))
    gu_term = dot(rows_all, pair_grad, (0, 0)).astype(BF)
    rows_grad = rows_grad.astype(BF)
    far, gu_term = lax.optimization_barrier((cross(rows_grad), gu_term))
    kept, came = send_rows(rows_grad, far)
    gu_term, down_sum, came = lax.optimization_barrier((gu_term, down_sum, came))
    gu_sum = lax.psum_scatter(gu_term, "z", scatter_dimension=0, tiled=True)
    ffn_part = dot(activation, down_t, (1, 1)).astype(BF)
    normed2_grad, ffn_part = lax.optimization_barrier((add_rows(kept, came), ffn_part))

    scaled_two = normed2_grad * gain_two
    middle_grad = cot.astype(F32) + inv_two * (
        scaled_two - normed_two * jnp.mean(scaled_two * normed_two, axis=-1, keepdims=True)
    )
    ffn_sums = near_sums(ffn_part, cross(ffn_part))
    middle_all, ffn_sums = gather_rows(middle_grad.astype(BF), ffn_sums)
    came = [swap(ffn_sums[k], CHIPS, k) for k in range(1, len(ffn_sums))]

    mixed_grad = dot(middle_all, out_mine, (1, 1))
    out_term = dot(mixed, middle_all, (0, 0)).astype(BF)
    cgate_grad = mixed_grad * conv
    conv_grad = mixed_grad * c_gate
    padded = jnp.concatenate([conv_grad.reshape(groups), from_piece(conv_grad, 0, 1)], axis=3)
    gated_grad = jnp.zeros(groups, F32)
    for offset in range(width):
        begin = rim - offset
        gated_grad = gated_grad + taps[offset] * padded[:, :, :, begin : begin + piece]
    gated_grad = gated_grad.reshape(-1, channels)
    taps_term = jnp.stack(
        [
            jnp.sum(
                conv_grad.reshape(groups) * extended[:, :, :, offset : offset + piece],
                axis=(0, 1, 2, 3),
            )
            for offset in range(width)
        ]
    )
    proj_grad = jnp.concatenate(
        [
            (gated_grad * x_value).astype(BF),
            cgate_grad.astype(BF),
            (gated_grad * b_gate).astype(BF),
        ],
        axis=1,
    )
    proj_grad, came = lax.optimization_barrier((proj_grad, came))
    block_out = middle + add_rows(ffn_sums[0], came)
    in_term = dot(hidden_one, proj_grad, (0, 0)).astype(BF)
    out_term = out_term.reshape(nz, sub, members, model // members)
    out_term = out_term.transpose(0, 2, 1, 3).reshape(nz, plane_rows, model // members)
    taps_term = taps_term.reshape(width, nz, sub).transpose(1, 0, 2)
    taps_term = jnp.pad(
        taps_term.astype(BF), ((0, 0), (0, 16 - width), (0, 3 * channels + out_width - sub))
    )
    last = jnp.concatenate([in_term.reshape(nz, plane_rows, 3 * channels), out_term], axis=2)
    last = jnp.concatenate([last, taps_term], axis=1)
    rows_grad = dot(proj_grad, in_mine, (1, 1)).astype(BF)
    last, gu_sum, far = lax.optimization_barrier((last, gu_sum, cross(rows_grad)))
    last = lax.psum_scatter(last, "z", scatter_dimension=0, tiled=True)[0]
    kept, came = send_rows(rows_grad, far)
    came, down_sum = lax.optimization_barrier((came, down_sum))
    down_came = exchange(down_sum.reshape(cells, rows, hidden), CELL)
    normed1_grad = add_rows(kept, came)
    normed_one = resid * inv_one
    scaled_one = normed1_grad * gain_one
    input_grad = middle_grad + inv_one * (
        scaled_one - normed_one * jnp.mean(scaled_one * normed_one, axis=-1, keepdims=True)
    )

    factor = 1.0 / math.sqrt(own * nz * members)
    down_out = jnp.concatenate(down_came, axis=1).T.astype(F32) * factor
    came = exchange(gu_sum.reshape(cells, rows, 2 * hidden), CELL)
    gu_out = jnp.stack(
        [
            jnp.concatenate([b[:, :hidden] for b in came], axis=1),
            jnp.concatenate([b[:, hidden:] for b in came], axis=1),
        ],
        axis=1,
    )
    gu_out = gu_out.astype(F32) * factor
    in_sum = last[:plane_rows, : 3 * channels]
    out_sum = last[:plane_rows, 3 * channels :].reshape(ny, cells, sub, out_width)
    out_sum = out_sum.transpose(0, 2, 1, 3).reshape(ny, sub, model // ny)
    out_out = jnp.concatenate(exchange(out_sum, "y"), axis=0).astype(F32) * factor
    taps_out = last[plane_rows : plane_rows + width, :sub].astype(F32) * factor

    start = z * plane_rows
    norm1_rows = jnp.sum(
        in_sum.astype(F32)
        * lax.dynamic_slice_in_dim(in_mine, start, plane_rows, 0).astype(F32),
        axis=1,
    ) / lax.dynamic_slice_in_dim(gain_one, start, plane_rows, 0)
    norm2_rows = jnp.sum(
        gu_sum.astype(F32) * gu_block.astype(F32), axis=1
    ) / lax.dynamic_slice_in_dim(gain_two, start, plane_rows, 0)
    norm_rows = jnp.stack([norm1_rows, norm2_rows]).reshape(2, cells, rows).transpose(1, 0, 2)
    norm_rows = thirds(norm_rows).transpose(1, 0, 2, 3).reshape(cells, 1, 6 * rows)
    extra = -(-6 * rows // lanes)
    extra = -(-extra // 16) * 16
    norm_rows = jnp.pad(norm_rows, ((0, 0), (0, 0), (0, extra * lanes - 6 * rows)))
    norm_rows = jnp.broadcast_to(norm_rows, (cells, ny, extra * lanes))
    norm_rows = norm_rows.reshape(members, extra, lanes)
    sent = in_sum.reshape(cells, 2, half, 3, channels).transpose(0, 3, 2, 1, 4)
    sent = dot(sent.reshape(cells * 3 * half, 2 * channels), take_order, (1, 1)).astype(BF)
    sent = sent.reshape(cells, 3 * half, ny, lanes).transpose(0, 2, 1, 3)
    sent = sent.reshape(members, 3 * half, lanes)
    came = plane_exchange(jnp.concatenate([sent, norm_rows], axis=1))
    norm_out = came[:, 3 * half :].reshape(members, extra * lanes)[:, : 6 * rows]
    norm_out = jnp.sum(norm_out.astype(F32).reshape(members * 3, 2, rows), axis=0)
    norm_out = lax.dynamic_slice_in_dim(norm_out, y * sub, sub, 1) * factor
    came = came[:, : 3 * half].transpose(1, 0, 2).reshape(3 * half, members * lanes)
    in_out = dot(came, send_order, (1, 1)).reshape(3, half, 2, cols)
    in_out = in_out.transpose(2, 1, 0, 3).reshape(rows, 3, cols) * factor

    return (
        block_out.reshape(tokens.shape),
        input_grad.reshape(tokens.shape),
        norm_out[0],
        in_out,
        taps_out,
        out_out,
        norm_out[1],
        gu_out,
        down_out,
    )


def solution(mesh):
    dp, seq = mesh.shape["dp"], mesh.shape["seq"]
    fine = Mesh(mesh.devices.reshape(dp // 4, 2, 2, seq), ("z", "x", "c", "y"))
    dp = ("z", "x", "c")
    every = ("z", "x", "c", "y")
    return jax.shard_map(
        local,
        mesh=fine,
        in_specs=(
            P(dp, "y", None),
            P(every),
            P(dp, None, "y"),
            P(None, every),
            P(dp, "y"),
            P(every),
            P(dp, None, "y"),
            P("y", dp),
            P(dp, "y", None),
        ),
        out_specs=(
            P(dp, "y", None),
            P(dp, "y", None),
            P(every),
            P(dp, None, "y"),
            P(None, every),
            P(dp, "y"),
            P(every),
            P(dp, None, "y"),
            P("y", dp),
        ),
        check_vma=False,
    )
```

```python
import math

import jax
import jax.numpy as jnp
from jax import lax
from jax.experimental.layout import Layout, with_layout_constraint
from jax.sharding import Mesh
from jax.sharding import PartitionSpec as P

epsilon = 1e-05
BF = jnp.bfloat16
F32 = jnp.float32
PLANE = ("x", "c", "y")
CHIPS = ("x", "y")
CELL = ("x", "c")


def size_of(axes):
    axes = (axes,) if isinstance(axes, str) else axes
    return math.prod(lax.axis_size(a) for a in axes)


def swap(block, axes, k):
    if k == 0:
        return block
    return lax.ppermute(block, axes, [(i, i ^ k) for i in range(size_of(axes))])


def pick(blocks, i):
    return lax.dynamic_index_in_dim(blocks, i, 0, keepdims=False)


def dot(a, b, dims=(1, 0)):
    return lax.dot_general(a, b, (((dims[0],), (dims[1],)), ((), ())), preferred_element_type=F32)


def exchange(blocks, axes):
    me = lax.axis_index(axes)
    n = size_of(axes)
    got = jnp.stack([swap(pick(blocks, me ^ k), axes, k) for k in range(n)])
    return [pick(got, me ^ j) for j in range(n)]


def rowwise(a):
    return with_layout_constraint(a, Layout(major_to_minor=(0, 1)))


def gather_rows(rows, beside=None):
    blocks = [swap(rows, CHIPS, k) for k in range(size_of(CHIPS))]
    if beside is not None:
        blocks, beside = lax.optimization_barrier((blocks, beside))
    near = lax.optimization_barrier(rowwise(jnp.concatenate(blocks, axis=0)))
    rows = jnp.concatenate([near, swap(near, "c", 1)], axis=0)
    return rows if beside is None else (rows, beside)


def cross(part):
    return swap(rowwise(part)[part.shape[0] // 2 :], "c", 1)


def near_sums(part, far):
    n = size_of(CHIPS)
    half = part.shape[0] // 2
    mine = part[:half].astype(F32) + far.astype(F32)
    mine = mine.reshape((n, half // n) + part.shape[1:])
    return [mine[0]] + [mine[k].astype(BF) for k in range(1, n)]


def send_rows(part, far):
    mine = near_sums(part, far)
    return mine[0], [swap(mine[k], CHIPS, k) for k in range(1, len(mine))]


def add_rows(mine, came):
    for block in came:
        mine = mine + block.astype(F32)
    return mine


def scatter_rows(part):
    return add_rows(*send_rows(part, cross(part)))


def plane_exchange(blocks):
    return lax.all_to_all(blocks, PLANE, 0, 0, tiled=True)


def thirds(a):
    high = lax.reduce_precision(a, 8, 7)
    rest = a - high
    mid = lax.reduce_precision(rest, 8, 7)
    return jnp.stack([high, mid, rest - mid]).astype(BF)


def whole(parts):
    parts = parts.astype(F32)
    return parts[0] + parts[1] + parts[2]


def lane_orders(zy, cells, ny, sub):
    n = zy * cells * ny * sub
    p = jnp.arange(2 * n).reshape(2, zy, cells, ny, sub).transpose(2, 3, 0, 1, 4).reshape(-1)
    m = 2 * ny * zy * sub
    q = jnp.arange(m).reshape(ny, 2, zy * sub).transpose(1, 0, 2).reshape(-1)
    send = (jnp.arange(2 * n)[:, None] == p[None, :]).astype(BF)
    take = (jnp.arange(m)[:, None] == q[None, :]).astype(BF)
    return send, take


def local(
    tokens,
    norm1_gain,
    in_weight,
    conv_weight,
    out_weight,
    norm2_gain,
    gate_up_weight,
    down_weight,
    cotangent,
):
    nz, nx, nc, ny = (size_of(a) for a in ("z", "x", "c", "y"))
    z, y = lax.axis_index("z"), lax.axis_index("y")
    cell = lax.axis_index(CELL)
    cells = nx * nc
    members = cells * ny
    rows = in_weight.shape[0]
    half = rows // 2
    sub = rows // ny
    zy = nz // ny
    width = conv_weight.shape[0]
    rim = width - 1
    seqs, piece, model = tokens.shape
    own = seqs * piece
    plane_rows = cells * rows
    hidden = gate_up_weight.shape[2] // cells
    channels = nz * sub
    cols = in_weight.shape[2]
    lanes = 2 * zy * sub
    tok = tokens.reshape(own, model)
    cot = cotangent.reshape(own, model)
    send_order, take_order = lane_orders(zy, cells, ny, sub)

    small = jnp.concatenate([norm1_gain[None], norm2_gain[None], conv_weight], axis=0)
    kinds = small.shape[0]
    small = thirds(small).reshape(-1)
    count = small.shape[0]
    extra = -(-count // (16 * lanes)) * 16
    small = jnp.pad(small, (0, extra * lanes - count)).reshape(1, extra, lanes)
    raw = in_weight.reshape(2, half, 3, cols).transpose(2, 1, 0, 3).reshape(3 * half, 2 * cols)
    sent = dot(raw, send_order).astype(BF).reshape(3 * half, members, lanes)
    sent = sent.transpose(1, 0, 2)
    sent = jnp.concatenate([sent, jnp.broadcast_to(small, (members, extra, lanes))], axis=1)
    with jax.named_scope("inmove"):
        came = plane_exchange(sent)
    held = came[:, 3 * half :].reshape(members, extra * lanes)[:, :count].reshape(-1)
    came = came[:, : 3 * half].reshape(cells, ny, 3 * half, lanes)
    came = came.transpose(0, 2, 1, 3).reshape(cells * 3 * half, ny * lanes)
    came = dot(came, take_order).astype(BF).reshape(cells, 3, half, 2, channels)
    in_block = came.transpose(0, 3, 2, 1, 4).reshape(plane_rows, 3 * channels)
    out_width = model // members
    out_block = exchange(out_weight.reshape(ny, sub, model // ny), "y")
    out_block = jnp.concatenate(
        [b[:, j * out_width : (j + 1) * out_width] for b in out_block for j in range(cells)], axis=0
    )
    first = jnp.concatenate([in_block, out_block], axis=1)
    wide = first.shape[1]
    rest = -(-members * count // (16 * wide)) * 16
    held = jnp.pad(held, (0, rest * wide - members * count)).reshape(rest, wide)
    first = jnp.concatenate([first, held], axis=0)
    with jax.named_scope("firstmove"):
        first = lax.all_gather(first, "z", axis=0, tiled=False)

    with jax.named_scope("tokmove"):
        tok_all = gather_rows(tok)

    down_rows = down_weight.T
    pieces = jnp.stack(
        [
            jnp.concatenate(
                [
                    w[:, j * hidden : (j + 1) * hidden]
                    for w in (gate_up_weight[:, 0], gate_up_weight[:, 1], down_rows)
                ],
                axis=1,
            )
            for j in range(cells)
        ]
    )
    ffn_block = jnp.concatenate(exchange(pieces, CELL), axis=0)
    gu_block, down_block, tok_all = lax.optimization_barrier(
        (ffn_block[:, : 2 * hidden], ffn_block[:, 2 * hidden :], tok_all)
    )
    gu_mine = lax.all_gather(gu_block, "z", axis=0, tiled=True)
    down_t = lax.all_gather(down_block, "z", axis=0, tiled=True)

    with jax.named_scope("cotmove"):
        cot_all = gather_rows(cot)
    held = first[:, plane_rows:].reshape(nz, rest * wide)[:, : members * count]
    held = held.reshape(nz, members, 3, kinds, sub).transpose(2, 3, 0, 1, 4)
    held = whole(held)
    gain_one = held[0].reshape(model)
    gain_two = held[1].reshape(model)
    taps = lax.dynamic_index_in_dim(held[2:], cell * ny + y, 2, keepdims=False)
    taps = taps.reshape(width, channels)
    in_mine = first[:, :plane_rows, : 3 * channels].reshape(model, 3 * channels)
    out_mine = first[:, :plane_rows, 3 * channels :].reshape(nz, members, sub, out_width)
    out_mine = out_mine.transpose(0, 2, 1, 3).reshape(channels, model)

    resid_all = tok_all.astype(F32)
    inv_all = lax.rsqrt(jnp.mean(resid_all * resid_all, axis=-1, keepdims=True) + epsilon)
    hidden_one = (resid_all * inv_all * gain_one).astype(BF)
    proj = dot(hidden_one, in_mine)
    b_gate = proj[:, :channels]
    c_gate = proj[:, channels : 2 * channels]
    x_value = proj[:, 2 * channels :]
    gated = (b_gate * x_value).astype(BF)

    groups = (nc * nx, ny, seqs, piece, channels)

    def from_piece(a, at, by):
        rows_of = a.reshape(groups)[:, :, :, at : at + rim]
        out = []
        for r in range(ny):
            v = jnp.zeros_like(rows_of[:, 0])
            for j in range(ny):
                v = jnp.where((y ^ r) + by == (y ^ j), rows_of[:, j], v)
            out.append(v)
        return jnp.stack(out, axis=1)

    extended = jnp.concatenate(
        [from_piece(gated, piece - rim, -1), gated.reshape(groups)], axis=3
    ).astype(F32)
    conv = jnp.zeros(groups, F32)
    for offset in range(width):
        conv = conv + taps[offset] * extended[:, :, :, offset : offset + piece]
    conv = conv.reshape(-1, channels)
    mixed = (c_gate * conv).astype(BF)
    resid = tok.astype(F32)
    inv_one = lax.rsqrt(jnp.mean(resid * resid, axis=-1, keepdims=True) + epsilon)
    middle = resid + scatter_rows(dot(mixed, out_mine).astype(BF))
    inv_two = lax.rsqrt(jnp.mean(middle * middle, axis=-1, keepdims=True) + epsilon)
    normed_two = middle * inv_two
    hidden_two = (normed_two * gain_two).astype(BF)
    rows_all = gather_rows(hidden_two)

    both = dot(rows_all, gu_mine)
    gate = both[:, :hidden]
    up = both[:, hidden:]
    sigma = jax.nn.sigmoid(gate)
    swish = gate * sigma
    activation = lax.optimization_barrier((swish * up).astype(BF))
    down_term = dot(cot_all, activation, (0, 0)).astype(BF)
    down_t, down_term = lax.optimization_barrier((down_t, down_term))
    down_sum = lax.psum_scatter(down_term, "z", scatter_dimension=0, tiled=True)
    act_grad = dot(cot_all, down_t)
    gate_grad = (act_grad * up * (sigma * (1.0 + gate * (1.0 - sigma)))).astype(BF)
    up_grad = (act_grad * swish).astype(BF)
    pair_grad = jnp.concatenate([gate_grad, up_grad], axis=1)
    rows_grad = dot(pair_grad, gu_mine, (1, 1))
    gu_term = dot(rows_all, pair_grad, (0, 0)).astype(BF)
    rows_grad = rows_grad.astype(BF)
    kept, came = send_rows(rows_grad, cross(rows_grad))
    gu_term, down_sum, came = lax.optimization_barrier((gu_term, down_sum, came))
    gu_sum = lax.psum_scatter(gu_term, "z", scatter_dimension=0, tiled=True)
    ffn_part = dot(activation, down_t, (1, 1)).astype(BF)
    normed2_grad, ffn_part = lax.optimization_barrier((add_rows(kept, came), ffn_part))

    scaled_two = normed2_grad * gain_two
    middle_grad = cot.astype(F32) + inv_two * (
        scaled_two - normed_two * jnp.mean(scaled_two * normed_two, axis=-1, keepdims=True)
    )
    ffn_sums = near_sums(ffn_part, cross(ffn_part))
    middle_all, ffn_sums = gather_rows(middle_grad.astype(BF), ffn_sums)
    came = [swap(ffn_sums[k], CHIPS, k) for k in range(1, len(ffn_sums))]

    mixed_grad = dot(middle_all, out_mine, (1, 1))
    out_term = dot(mixed, middle_all, (0, 0)).astype(BF)
    cgate_grad = mixed_grad * conv
    conv_grad = mixed_grad * c_gate
    padded = jnp.concatenate([conv_grad.reshape(groups), from_piece(conv_grad, 0, 1)], axis=3)
    gated_grad = jnp.zeros(groups, F32)
    for offset in range(width):
        begin = rim - offset
        gated_grad = gated_grad + taps[offset] * padded[:, :, :, begin : begin + piece]
    gated_grad = gated_grad.reshape(-1, channels)
    taps_term = jnp.stack(
        [
            jnp.sum(
                conv_grad.reshape(groups) * extended[:, :, :, offset : offset + piece],
                axis=(0, 1, 2, 3),
            )
            for offset in range(width)
        ]
    )
    proj_grad = jnp.concatenate(
        [
            (gated_grad * x_value).astype(BF),
            cgate_grad.astype(BF),
            (gated_grad * b_gate).astype(BF),
        ],
        axis=1,
    )
    proj_grad, came = lax.optimization_barrier((proj_grad, came))
    block_out = middle + add_rows(ffn_sums[0], came)
    in_term = dot(hidden_one, proj_grad, (0, 0)).astype(BF)
    out_term = out_term.reshape(nz, sub, members, model // members)
    out_term = out_term.transpose(0, 2, 1, 3).reshape(nz, plane_rows, model // members)
    taps_term = taps_term.reshape(width, nz, sub).transpose(1, 0, 2)
    taps_term = jnp.pad(
        taps_term.astype(BF), ((0, 0), (0, 16 - width), (0, 3 * channels + out_width - sub))
    )
    last = jnp.concatenate([in_term.reshape(nz, plane_rows, 3 * channels), out_term], axis=2)
    last = jnp.concatenate([last, taps_term], axis=1)
    rows_grad = dot(proj_grad, in_mine, (1, 1)).astype(BF)
    last, gu_sum, far, down_sum = lax.optimization_barrier(
        (last, gu_sum, cross(rows_grad), down_sum)
    )
    last = lax.psum_scatter(last, "z", scatter_dimension=0, tiled=True)[0]
    kept, came = send_rows(rows_grad, far)
    normed1_grad = add_rows(kept, came)
    normed_one = resid * inv_one
    scaled_one = normed1_grad * gain_one
    input_grad = middle_grad + inv_one * (
        scaled_one - normed_one * jnp.mean(scaled_one * normed_one, axis=-1, keepdims=True)
    )

    factor = 1.0 / math.sqrt(own * nz * members)
    ffn_sum = jnp.concatenate([gu_sum, down_sum], axis=1).reshape(cells, rows, 3 * hidden)
    came = lax.all_to_all(ffn_sum, CELL, 0, 0, tiled=True)
    down_out = jnp.concatenate([b[:, 2 * hidden :] for b in came], axis=1).T
    down_out = down_out.astype(F32) * factor
    gu_out = jnp.stack(
        [
            jnp.concatenate([b[:, :hidden] for b in came], axis=1),
            jnp.concatenate([b[:, hidden : 2 * hidden] for b in came], axis=1),
        ],
        axis=1,
    )
    gu_out = gu_out.astype(F32) * factor
    in_sum = last[:plane_rows, : 3 * channels]
    out_sum = last[:plane_rows, 3 * channels :].reshape(ny, cells, sub, out_width)
    out_sum = out_sum.transpose(0, 2, 1, 3).reshape(ny, sub, model // ny)
    out_out = jnp.concatenate(exchange(out_sum, "y"), axis=0).astype(F32) * factor
    taps_out = last[plane_rows : plane_rows + width, :sub].astype(F32) * factor

    start = z * plane_rows
    norm1_rows = jnp.sum(
        in_sum.astype(F32)
        * lax.dynamic_slice_in_dim(in_mine, start, plane_rows, 0).astype(F32),
        axis=1,
    ) / lax.dynamic_slice_in_dim(gain_one, start, plane_rows, 0)
    norm2_rows = jnp.sum(
        gu_sum.astype(F32) * gu_block.astype(F32), axis=1
    ) / lax.dynamic_slice_in_dim(gain_two, start, plane_rows, 0)
    norm_rows = jnp.stack([norm1_rows, norm2_rows]).reshape(2, cells, rows).transpose(1, 0, 2)
    norm_rows = thirds(norm_rows).transpose(1, 0, 2, 3).reshape(cells, 1, 6 * rows)
    extra = -(-6 * rows // lanes)
    extra = -(-extra // 16) * 16
    norm_rows = jnp.pad(norm_rows, ((0, 0), (0, 0), (0, extra * lanes - 6 * rows)))
    norm_rows = jnp.broadcast_to(norm_rows, (cells, ny, extra * lanes))
    norm_rows = norm_rows.reshape(members, extra, lanes)
    sent = in_sum.reshape(cells, 2, half, 3, channels).transpose(0, 3, 2, 1, 4)
    sent = dot(sent.reshape(cells * 3 * half, 2 * channels), take_order, (1, 1)).astype(BF)
    sent = sent.reshape(cells, 3 * half, ny, lanes).transpose(0, 2, 1, 3)
    sent = sent.reshape(members, 3 * half, lanes)
    came = plane_exchange(jnp.concatenate([sent, norm_rows], axis=1))
    norm_out = came[:, 3 * half :].reshape(members, extra * lanes)[:, : 6 * rows]
    norm_out = jnp.sum(norm_out.astype(F32).reshape(members * 3, 2, rows), axis=0)
    norm_out = lax.dynamic_slice_in_dim(norm_out, y * sub, sub, 1) * factor
    came = came[:, : 3 * half].transpose(1, 0, 2).reshape(3 * half, members * lanes)
    in_out = dot(came, send_order, (1, 1)).reshape(3, half, 2, cols)
    in_out = in_out.transpose(2, 1, 0, 3).reshape(rows, 3, cols) * factor

    return (
        block_out.reshape(tokens.shape),
        input_grad.reshape(tokens.shape),
        norm_out[0],
        in_out,
        taps_out,
        out_out,
        norm_out[1],
        gu_out,
        down_out,
    )


def solution(mesh):
    dp, seq = mesh.shape["dp"], mesh.shape["seq"]
    fine = Mesh(mesh.devices.reshape(dp // 4, 2, 2, seq), ("z", "x", "c", "y"))
    dp = ("z", "x", "c")
    every = ("z", "x", "c", "y")
    return jax.shard_map(
        local,
        mesh=fine,
        in_specs=(
            P(dp, "y", None),
            P(every),
            P(dp, None, "y"),
            P(None, every),
            P(dp, "y"),
            P(every),
            P(dp, None, "y"),
            P("y", dp),
            P(dp, "y", None),
        ),
        out_specs=(
            P(dp, "y", None),
            P(dp, "y", None),
            P(every),
            P(dp, None, "y"),
            P(None, every),
            P(dp, "y"),
            P(every),
            P(dp, None, "y"),
            P("y", dp),
        ),
        check_vma=False,
    )
```

```python
import math

import jax
import jax.numpy as jnp
from jax import lax
from jax.experimental.layout import Layout, with_layout_constraint
from jax.sharding import Mesh
from jax.sharding import PartitionSpec as P

epsilon = 1e-05
BF = jnp.bfloat16
F32 = jnp.float32
PLANE = ("x", "c", "y")
CHIPS = ("x", "y")
CELL = ("x", "c")


def size_of(axes):
    axes = (axes,) if isinstance(axes, str) else axes
    return math.prod(lax.axis_size(a) for a in axes)


def swap(block, axes, k):
    if k == 0:
        return block
    return lax.ppermute(block, axes, [(i, i ^ k) for i in range(size_of(axes))])


def pick(blocks, i):
    return lax.dynamic_index_in_dim(blocks, i, 0, keepdims=False)


def dot(a, b, dims=(1, 0)):
    return lax.dot_general(a, b, (((dims[0],), (dims[1],)), ((), ())), preferred_element_type=F32)


def exchange(blocks, axes):
    me = lax.axis_index(axes)
    n = size_of(axes)
    got = jnp.stack([swap(pick(blocks, me ^ k), axes, k) for k in range(n)])
    return [pick(got, me ^ j) for j in range(n)]


def rowwise(a):
    return with_layout_constraint(a, Layout(major_to_minor=(0, 1)))


def gather_rows(rows, beside=None):
    blocks = [swap(rows, CHIPS, k) for k in range(size_of(CHIPS))]
    if beside is not None:
        blocks, beside = lax.optimization_barrier((blocks, beside))
    near = lax.optimization_barrier(rowwise(jnp.concatenate(blocks, axis=0)))
    rows = jnp.concatenate([near, swap(near, "c", 1)], axis=0)
    return rows if beside is None else (rows, beside)


def cross(part):
    return swap(rowwise(part)[part.shape[0] // 2 :], "c", 1)


def near_sums(part, far):
    n = size_of(CHIPS)
    half = part.shape[0] // 2
    mine = part[:half].astype(F32) + far.astype(F32)
    mine = mine.reshape((n, half // n) + part.shape[1:])
    return [mine[0]] + [mine[k].astype(BF) for k in range(1, n)]


def send_rows(part, far):
    mine = near_sums(part, far)
    return mine[0], [swap(mine[k], CHIPS, k) for k in range(1, len(mine))]


def add_rows(mine, came):
    for block in came:
        mine = mine + block.astype(F32)
    return mine


def scatter_rows(part):
    return add_rows(*send_rows(part, cross(part)))


def plane_exchange(blocks):
    return lax.all_to_all(blocks, PLANE, 0, 0, tiled=True)


def thirds(a):
    high = lax.reduce_precision(a, 8, 7)
    rest = a - high
    mid = lax.reduce_precision(rest, 8, 7)
    return jnp.stack([high, mid, rest - mid]).astype(BF)


def whole(parts):
    parts = parts.astype(F32)
    return parts[0] + parts[1] + parts[2]


def lane_orders(zy, cells, ny, sub):
    n = zy * cells * ny * sub
    p = jnp.arange(2 * n).reshape(2, zy, cells, ny, sub).transpose(2, 3, 0, 1, 4).reshape(-1)
    m = 2 * ny * zy * sub
    q = jnp.arange(m).reshape(ny, 2, zy * sub).transpose(1, 0, 2).reshape(-1)
    send = (jnp.arange(2 * n)[:, None] == p[None, :]).astype(BF)
    take = (jnp.arange(m)[:, None] == q[None, :]).astype(BF)
    return send, take


def local(
    tokens,
    norm1_gain,
    in_weight,
    conv_weight,
    out_weight,
    norm2_gain,
    gate_up_weight,
    down_weight,
    cotangent,
):
    nz, nx, nc, ny = (size_of(a) for a in ("z", "x", "c", "y"))
    z, y = lax.axis_index("z"), lax.axis_index("y")
    cell = lax.axis_index(CELL)
    cells = nx * nc
    members = cells * ny
    rows = in_weight.shape[0]
    half = rows // 2
    sub = rows // ny
    zy = nz // ny
    width = conv_weight.shape[0]
    rim = width - 1
    seqs, piece, model = tokens.shape
    own = seqs * piece
    plane_rows = cells * rows
    hidden = gate_up_weight.shape[2] // cells
    channels = nz * sub
    cols = in_weight.shape[2]
    lanes = 2 * zy * sub
    tok = tokens.reshape(own, model)
    cot = cotangent.reshape(own, model)
    send_order, take_order = lane_orders(zy, cells, ny, sub)

    small = jnp.concatenate([norm1_gain[None], norm2_gain[None], conv_weight], axis=0)
    kinds = small.shape[0]
    small = thirds(small).reshape(-1)
    count = small.shape[0]
    extra = -(-count // (16 * lanes)) * 16
    small = jnp.pad(small, (0, extra * lanes - count)).reshape(1, extra, lanes)
    raw = in_weight.reshape(2, half, 3, cols).transpose(2, 1, 0, 3).reshape(3 * half, 2 * cols)
    sent = dot(raw, send_order).astype(BF).reshape(3 * half, members, lanes)
    sent = sent.transpose(1, 0, 2)
    sent = jnp.concatenate([sent, jnp.broadcast_to(small, (members, extra, lanes))], axis=1)
    with jax.named_scope("inmove"):
        came = plane_exchange(sent)
    held = came[:, 3 * half :].reshape(members, extra * lanes)[:, :count].reshape(-1)
    came = came[:, : 3 * half].reshape(cells, ny, 3 * half, lanes)
    came = came.transpose(0, 2, 1, 3).reshape(cells * 3 * half, ny * lanes)
    came = dot(came, take_order).astype(BF).reshape(cells, 3, half, 2, channels)
    in_block = came.transpose(0, 3, 2, 1, 4).reshape(plane_rows, 3 * channels)
    out_width = model // members
    out_block = jnp.concatenate(
        [out_weight[:, j * out_width : (j + 1) * out_width] for j in range(cells)], axis=0
    )
    first = jnp.concatenate([in_block, out_block], axis=1)
    wide = first.shape[1]
    rest = -(-members * count // (16 * wide)) * 16
    held = jnp.pad(held, (0, rest * wide - members * count)).reshape(rest, wide)
    first = jnp.concatenate([first, held], axis=0)
    with jax.named_scope("firstmove"):
        first = lax.all_gather(first, "z", axis=0, tiled=False)

    with jax.named_scope("tokmove"):
        tok_all = gather_rows(tok)

    down_rows = down_weight.T
    pieces = jnp.stack(
        [
            jnp.concatenate(
                [
                    w[:, j * hidden : (j + 1) * hidden]
                    for w in (gate_up_weight[:, 0], gate_up_weight[:, 1], down_rows)
                ],
                axis=1,
            )
            for j in range(cells)
        ]
    )
    ffn_block = jnp.concatenate(exchange(pieces, CELL), axis=0)
    gu_block, down_block, tok_all = lax.optimization_barrier(
        (ffn_block[:, : 2 * hidden], ffn_block[:, 2 * hidden :], tok_all)
    )
    gu_mine = lax.all_gather(gu_block, "z", axis=0, tiled=True)
    down_t = lax.all_gather(down_block, "z", axis=0, tiled=True)

    with jax.named_scope("cotmove"):
        cot_all = gather_rows(cot)
    held = first[:, plane_rows:].reshape(nz, rest * wide)[:, : members * count]
    held = held.reshape(nz, members, 3, kinds, sub).transpose(2, 3, 0, 1, 4)
    held = whole(held)
    gain_one = held[0].reshape(model)
    gain_two = held[1].reshape(model)
    taps = lax.dynamic_index_in_dim(held[2:], cell * ny + y, 2, keepdims=False)
    taps = taps.reshape(width, channels)
    in_mine = first[:, :plane_rows, : 3 * channels].reshape(model, 3 * channels)
    out_raw = first[:, :plane_rows, 3 * channels :].reshape(nz, cells, ny, sub, out_width)
    out_raw = out_raw.transpose(2, 0, 3, 1, 4).reshape(ny, channels, model // ny)
    out_mine = jnp.concatenate(exchange(out_raw, "y"), axis=1)

    resid_all = tok_all.astype(F32)
    inv_all = lax.rsqrt(jnp.mean(resid_all * resid_all, axis=-1, keepdims=True) + epsilon)
    hidden_one = (resid_all * inv_all * gain_one).astype(BF)
    proj = dot(hidden_one, in_mine)
    b_gate = proj[:, :channels]
    c_gate = proj[:, channels : 2 * channels]
    x_value = proj[:, 2 * channels :]
    gated = (b_gate * x_value).astype(BF)

    groups = (nc * nx, ny, seqs, piece, channels)

    def from_piece(a, at, by):
        rows_of = a.reshape(groups)[:, :, :, at : at + rim]
        out = []
        for r in range(ny):
            v = jnp.zeros_like(rows_of[:, 0])
            for j in range(ny):
                v = jnp.where((y ^ r) + by == (y ^ j), rows_of[:, j], v)
            out.append(v)
        return jnp.stack(out, axis=1)

    extended = jnp.concatenate(
        [from_piece(gated, piece - rim, -1), gated.reshape(groups)], axis=3
    ).astype(F32)
    conv = jnp.zeros(groups, F32)
    for offset in range(width):
        conv = conv + taps[offset] * extended[:, :, :, offset : offset + piece]
    conv = conv.reshape(-1, channels)
    mixed = (c_gate * conv).astype(BF)
    resid = tok.astype(F32)
    inv_one = lax.rsqrt(jnp.mean(resid * resid, axis=-1, keepdims=True) + epsilon)
    middle = resid + scatter_rows(dot(mixed, out_mine).astype(BF))
    inv_two = lax.rsqrt(jnp.mean(middle * middle, axis=-1, keepdims=True) + epsilon)
    normed_two = middle * inv_two
    hidden_two = (normed_two * gain_two).astype(BF)
    rows_all = gather_rows(hidden_two)

    both = dot(rows_all, gu_mine)
    gate = both[:, :hidden]
    up = both[:, hidden:]
    sigma = jax.nn.sigmoid(gate)
    swish = gate * sigma
    activation = lax.optimization_barrier((swish * up).astype(BF))
    down_term = dot(cot_all, activation, (0, 0)).astype(BF)
    down_t, down_term = lax.optimization_barrier((down_t, down_term))
    down_sum = lax.psum_scatter(down_term, "z", scatter_dimension=0, tiled=True)
    act_grad = dot(cot_all, down_t)
    gate_grad = (act_grad * up * (sigma * (1.0 + gate * (1.0 - sigma)))).astype(BF)
    up_grad = (act_grad * swish).astype(BF)
    pair_grad = jnp.concatenate([gate_grad, up_grad], axis=1)
    rows_grad = dot(pair_grad, gu_mine, (1, 1))
    gu_term = dot(rows_all, pair_grad, (0, 0)).astype(BF)
    rows_grad = rows_grad.astype(BF)
    kept, came = send_rows(rows_grad, cross(rows_grad))
    gu_term, down_sum, came = lax.optimization_barrier((gu_term, down_sum, came))
    gu_sum = lax.psum_scatter(gu_term, "z", scatter_dimension=0, tiled=True)
    ffn_part = dot(activation, down_t, (1, 1)).astype(BF)
    normed2_grad, ffn_part = lax.optimization_barrier((add_rows(kept, came), ffn_part))

    scaled_two = normed2_grad * gain_two
    middle_grad = cot.astype(F32) + inv_two * (
        scaled_two - normed_two * jnp.mean(scaled_two * normed_two, axis=-1, keepdims=True)
    )
    ffn_sums = near_sums(ffn_part, cross(ffn_part))
    middle_all, ffn_sums = gather_rows(middle_grad.astype(BF), ffn_sums)
    came = [swap(ffn_sums[k], CHIPS, k) for k in range(1, len(ffn_sums))]

    mixed_grad = dot(middle_all, out_mine, (1, 1))
    out_term = dot(mixed, middle_all, (0, 0)).astype(BF)
    cgate_grad = mixed_grad * conv
    conv_grad = mixed_grad * c_gate
    padded = jnp.concatenate([conv_grad.reshape(groups), from_piece(conv_grad, 0, 1)], axis=3)
    gated_grad = jnp.zeros(groups, F32)
    for offset in range(width):
        begin = rim - offset
        gated_grad = gated_grad + taps[offset] * padded[:, :, :, begin : begin + piece]
    gated_grad = gated_grad.reshape(-1, channels)
    taps_term = jnp.stack(
        [
            jnp.sum(
                conv_grad.reshape(groups) * extended[:, :, :, offset : offset + piece],
                axis=(0, 1, 2, 3),
            )
            for offset in range(width)
        ]
    )
    proj_grad = jnp.concatenate(
        [
            (gated_grad * x_value).astype(BF),
            cgate_grad.astype(BF),
            (gated_grad * b_gate).astype(BF),
        ],
        axis=1,
    )
    proj_grad, came = lax.optimization_barrier((proj_grad, came))
    block_out = middle + add_rows(ffn_sums[0], came)
    in_term = dot(hidden_one, proj_grad, (0, 0)).astype(BF)
    out_term = out_term.reshape(nz, sub, members, model // members)
    out_term = out_term.transpose(0, 2, 1, 3).reshape(nz, plane_rows, model // members)
    taps_term = taps_term.reshape(width, nz, sub).transpose(1, 0, 2)
    taps_term = jnp.pad(
        taps_term.astype(BF), ((0, 0), (0, 16 - width), (0, 3 * channels + out_width - sub))
    )
    last = jnp.concatenate([in_term.reshape(nz, plane_rows, 3 * channels), out_term], axis=2)
    last = jnp.concatenate([last, taps_term], axis=1)
    rows_grad = dot(proj_grad, in_mine, (1, 1)).astype(BF)
    last, gu_sum, far, down_sum = lax.optimization_barrier(
        (last, gu_sum, cross(rows_grad), down_sum)
    )
    last = lax.psum_scatter(last, "z", scatter_dimension=0, tiled=True)[0]
    kept, came = send_rows(rows_grad, far)
    normed1_grad = add_rows(kept, came)
    normed_one = resid * inv_one
    scaled_one = normed1_grad * gain_one
    input_grad = middle_grad + inv_one * (
        scaled_one - normed_one * jnp.mean(scaled_one * normed_one, axis=-1, keepdims=True)
    )

    factor = 1.0 / math.sqrt(own * nz * members)
    ffn_sum = jnp.concatenate([gu_sum, down_sum], axis=1).reshape(cells, rows, 3 * hidden)
    came = lax.all_to_all(ffn_sum, CELL, 0, 0, tiled=True)
    down_out = jnp.concatenate([b[:, 2 * hidden :] for b in came], axis=1).T
    down_out = down_out.astype(F32) * factor
    gu_out = jnp.stack(
        [
            jnp.concatenate([b[:, :hidden] for b in came], axis=1),
            jnp.concatenate([b[:, hidden : 2 * hidden] for b in came], axis=1),
        ],
        axis=1,
    )
    gu_out = gu_out.astype(F32) * factor
    in_sum = last[:plane_rows, : 3 * channels]
    start = z * plane_rows
    norm1_rows = jnp.sum(
        in_sum.astype(F32)
        * lax.dynamic_slice_in_dim(in_mine, start, plane_rows, 0).astype(F32),
        axis=1,
    ) / lax.dynamic_slice_in_dim(gain_one, start, plane_rows, 0)
    norm2_rows = jnp.sum(
        gu_sum.astype(F32) * gu_block.astype(F32), axis=1
    ) / lax.dynamic_slice_in_dim(gain_two, start, plane_rows, 0)
    norm_rows = jnp.stack([norm1_rows, norm2_rows]).reshape(2, cells, rows).transpose(1, 0, 2)
    norm_rows = thirds(norm_rows).transpose(1, 0, 2, 3).reshape(cells, 1, 6 * rows)
    extra = -(-6 * rows // lanes)
    extra = -(-extra // 16) * 16
    norm_rows = jnp.pad(norm_rows, ((0, 0), (0, 0), (0, extra * lanes - 6 * rows)))
    norm_rows = jnp.broadcast_to(norm_rows, (cells, ny, extra * lanes))
    norm_rows = norm_rows.reshape(members, extra, lanes)
    sent = in_sum.reshape(cells, 2, half, 3, channels).transpose(0, 3, 2, 1, 4)
    sent = dot(sent.reshape(cells * 3 * half, 2 * channels), take_order, (1, 1)).astype(BF)
    sent = sent.reshape(cells, 3 * half, ny, lanes).transpose(0, 2, 1, 3)
    sent = sent.reshape(members, 3 * half, lanes)
    sent, last = lax.optimization_barrier((jnp.concatenate([sent, norm_rows], axis=1), last))
    came = plane_exchange(sent)
    out_sum = last[:plane_rows, 3 * channels :].reshape(ny, cells, sub, out_width)
    out_sum = out_sum.transpose(0, 2, 1, 3).reshape(ny, sub, model // ny)
    out_out = jnp.concatenate(exchange(out_sum, "y"), axis=0).astype(F32) * factor
    taps_out = last[plane_rows : plane_rows + width, :sub].astype(F32) * factor
    norm_out = came[:, 3 * half :].reshape(members, extra * lanes)[:, : 6 * rows]
    norm_out = jnp.sum(norm_out.astype(F32).reshape(members * 3, 2, rows), axis=0)
    norm_out = lax.dynamic_slice_in_dim(norm_out, y * sub, sub, 1) * factor
    came = came[:, : 3 * half].transpose(1, 0, 2).reshape(3 * half, members * lanes)
    in_out = dot(came, send_order, (1, 1)).reshape(3, half, 2, cols)
    in_out = in_out.transpose(2, 1, 0, 3).reshape(rows, 3, cols) * factor

    return (
        block_out.reshape(tokens.shape),
        input_grad.reshape(tokens.shape),
        norm_out[0],
        in_out,
        taps_out,
        out_out,
        norm_out[1],
        gu_out,
        down_out,
    )


def solution(mesh):
    dp, seq = mesh.shape["dp"], mesh.shape["seq"]
    fine = Mesh(mesh.devices.reshape(dp // 4, 2, 2, seq), ("z", "x", "c", "y"))
    dp = ("z", "x", "c")
    every = ("z", "x", "c", "y")
    return jax.shard_map(
        local,
        mesh=fine,
        in_specs=(
            P(dp, "y", None),
            P(every),
            P(dp, None, "y"),
            P(None, every),
            P(dp, "y"),
            P(every),
            P(dp, None, "y"),
            P("y", dp),
            P(dp, "y", None),
        ),
        out_specs=(
            P(dp, "y", None),
            P(dp, "y", None),
            P(every),
            P(dp, None, "y"),
            P(None, every),
            P(dp, "y"),
            P(every),
            P(dp, None, "y"),
            P("y", dp),
        ),
        check_vma=False,
    )
```
